32 devices in a mesh: frame: 8 (over y, x, core), tensor: 4 (over z).
Axes of the slice: x: 2, y: 2, z: 4, core: 2. Of those that a mesh axis runs over, the one named last changes fastest.
Arguments:
- tokens: bfloat16 [1024, 1, 4096], P(('frame', 'tensor')), may hold values from -6 to 6
- norm_gain: float32 [4096], replicated, may hold values from 0.5 to 1.5
- query_weight: bfloat16 [4096, 4096], P(None, 'tensor'), may hold values from -0.09375 to 0.09375
- out_weight: bfloat16 [4096, 4096], P('tensor'), may hold values from -0.09375 to 0.09375
- cache_keys: bfloat16 [384, 1, 4096], P('frame', None, 'tensor'), may hold values from -420 to 420
- cache_values: bfloat16 [384, 1, 4096], P('frame', None, 'tensor'), may hold values from -18 to 18
- token_pos: int32 [1024, 1], P('frame'), may hold values from 0 to 383, as said below
- frame_pad: int32 [1], replicated, may hold values from 0 to 192
Outputs:
- mixed: bfloat16 [1024, 1, 4096], P(('frame', 'tensor'))
The draws below stay inside these ranges and needn't reach their ends.
Inputs may be any that keep to these rules, and one draw needn't show every extreme that they name: `token_pos`: nondecreasing along each sequence; the last token of every sequence has 383.
All inputs are finite; a program needn't handle non-finite values.
Results may differ from the reference program's by a relative error of at most 0.018.
Values may be sent and summed in bfloat16 or wider, within the bound.
A program may use at most 64 MiB of HBM per device.

```python
import jax
import jax.numpy as jnp
from jax import lax

D = 4096
HEADS = 32
HEAD_DIM = 128
SEQS = 1
LENGTH = 1024
FRAMES = 384
N_TENSOR = 4


def draw_token_pos(key, part):
    climbs = jax.random.randint(jax.random.fold_in(key, 11), (LENGTH, SEQS), 0, 3)
    climbed = jnp.cumsum(climbs, axis=0)
    placed = jnp.minimum(climbed * FRAMES // LENGTH, FRAMES - 1)
    finals = jnp.arange(LENGTH)[:, None] == LENGTH - 1
    return jnp.where(finals, FRAMES - 1, placed).astype(jnp.int32)


def draw_cache_keys(key, part):
    shape = (FRAMES, SEQS, HEADS * HEAD_DIM)
    base = 2.0 * jax.random.normal(jax.random.fold_in(key, 23), shape, jnp.float32)
    return jnp.clip(base, -12.0, 12.0).astype(jnp.bfloat16)


def block_scale(stream_key, extent, shards, smallest, top_value):
    level, own = 1.0, jax.random.fold_in(stream_key, 6)
    for dim, blocks in shards:
        draws = jnp.exp(jax.random.uniform(jax.random.fold_in(own, dim), (blocks,), jnp.float32, smallest / len(shards), top_value / len(shards)))
        level = level * jnp.repeat(draws, extent[dim] // blocks).reshape([-1 if axis == dim else 1 for axis in range(len(extent))])
    return level


def bell_draw(key, dims, spread, bound, split=(), kind=jnp.bfloat16):
    drawn = spread * jax.random.normal(key, dims, jnp.float32)
    if split:
        drawn = drawn * block_scale(key, dims, split, -0.22, 0.18)
    return jnp.clip(drawn, -bound, bound).astype(kind)


def setup_inputs(seed: int = 0) -> dict:
    keys = jax.random.split(jax.random.key(seed), 9)
    tokens = bell_draw(keys[0], (LENGTH, SEQS, D), 1.0, 6.0, ((0, 32),))
    norm_gain = jnp.clip(1.0 + 0.1 * jax.random.normal(keys[1], (D,), jnp.float32), 0.5, 1.5)
    query_weight = bell_draw(keys[2], (D, HEADS * HEAD_DIM), D ** -0.5, 0.09375, ((1, 4),))
    out_weight = bell_draw(keys[3], (HEADS * HEAD_DIM, D), (HEADS * HEAD_DIM) ** -0.5, 0.09375, ((0, 4),))
    cache_keys = draw_cache_keys(jax.random.fold_in(keys[8], 71), 0)
    cache_values = bell_draw(keys[5], (FRAMES, SEQS, HEADS * HEAD_DIM), 3.0, 18.0, ((0, 8), (2, 4)))
    token_pos = draw_token_pos(jax.random.fold_in(keys[8], 71), 0)
    frame_pad = jax.random.randint(keys[7], (SEQS,), 0, FRAMES // 2 + 1).astype(jnp.int32)
    return {"tokens": tokens, "norm_gain": norm_gain, "query_weight": query_weight, "out_weight": out_weight, "cache_keys": cache_keys, "cache_values": cache_values, "token_pos": token_pos, "frame_pad": frame_pad}


epsilon = 1e-06
masked_score = -1e+30

def reference(tokens, norm_gain, query_weight, out_weight, cache_keys, cache_values, token_pos, frame_pad):
    hidden = tokens.astype(jnp.float32)
    factor = lax.rsqrt(lax.optimization_barrier(jnp.mean(hidden * hidden, axis=-1, keepdims=True)) + epsilon)
    normed = (hidden * factor * norm_gain.astype(jnp.float32)).astype(jnp.bfloat16)
    queries = (jnp.dot(normed, query_weight, preferred_element_type=jnp.float32) * HEAD_DIM ** (-0.5)).astype(jnp.bfloat16)
    frame_index = jnp.arange(FRAMES, dtype=jnp.int32)
    valid_frames = (FRAMES - frame_pad).astype(jnp.int32)
    visible = (frame_index[None, :, None] <= token_pos[:, None, :]) & (frame_index[None, :, None] < valid_frames[None, None, :])
    query_heads = queries.reshape(LENGTH, SEQS, HEADS, HEAD_DIM).transpose(2, 0, 1, 3)
    key_heads = cache_keys.reshape(FRAMES, SEQS, HEADS, HEAD_DIM).transpose(2, 0, 1, 3)
    value_heads = cache_values.reshape(FRAMES, SEQS, HEADS, HEAD_DIM).transpose(2, 0, 1, 3)

    def one_head(operands):
        query_one, key_one, value_one = operands
        scores = jnp.einsum('lsd,fsd->lfs', query_one.astype(jnp.float32), key_one.astype(jnp.float32))
        scores = jnp.where(visible, scores, masked_score)
        highest = lax.optimization_barrier(jnp.max(scores, axis=1, keepdims=True))
        weights = jnp.where(visible, jnp.exp(scores - highest), 0.0)
        summed = lax.optimization_barrier(jnp.sum(weights, axis=1))
        rounded = lax.optimization_barrier(weights.astype(jnp.bfloat16)).astype(jnp.float32)
        gathered = jnp.einsum('lfs,fsd->lsd', rounded, value_one.astype(jnp.float32))
        return (gathered / summed[:, :, None]).astype(jnp.bfloat16)
    attended = lax.map(one_head, (query_heads, key_heads, value_heads))
    per_group = HEADS // N_TENSOR
    groups = attended.reshape(N_TENSOR, per_group, LENGTH, SEQS, HEAD_DIM).transpose(0, 2, 3, 1, 4)
    groups = groups.reshape(N_TENSOR, LENGTH, SEQS, per_group * HEAD_DIM)
    weight_groups = out_weight.reshape(N_TENSOR, per_group * HEAD_DIM, D)

    def add_group(running, operands):
        head_group, weight_group = operands
        partial_value = jnp.dot(head_group, weight_group, preferred_element_type=jnp.float32)
        partial_value = lax.optimization_barrier(partial_value.astype(jnp.bfloat16)).astype(jnp.float32)
        return (running + partial_value, None)
    summed_out, _ = lax.scan(add_group, jnp.zeros((LENGTH, SEQS, D), jnp.float32), (groups, weight_groups))
    return summed_out.astype(jnp.bfloat16)
```

```python
import functools
import math

import jax
import jax.numpy as jnp
from jax import lax
from jax.experimental import pallas as pl
from jax.experimental.pallas import tpu as pltpu
from jax.sharding import PartitionSpec as P

HEAD_DIM = 128
epsilon = 1e-06
masked_score = -1e30
MESH = pl.DeviceIdType.MESH


def flip(index, bit):
    return index + bit - 2 * bit * lax.rem(lax.div(index, bit), 2)


def kernel(
    n, frames_n, q_tile, o_tile, parts,
    tok, gain, wq_hbm, wo_hbm, keys, values, pos, pad,
    out,
    wq, wo, kg, vg, xg, nbuf, qbuf, abuf, pbuf, rbuf,
    load_sem, own_sem, kv_own, k_send, k_recv, v_send, v_recv,
    x_send, x_recv, p_send, p_recv,
):
    me_f = lax.axis_index("frame")
    me = lax.axis_index("tensor")
    rows = tok.shape[0]
    width = tok.shape[1]
    cols = wq.shape[1]
    span = keys.shape[0]
    bits = [1 << b for b in range(int(math.log2(frames_n)))][::-1]
    k_order = bits
    v_order = bits[1::-1] + bits[2:] if len(bits) > 1 else bits
    n_out = width // o_tile

    def load(src, dst, slot, part):
        depth = dst.shape[0] // parts
        window = pl.ds(part * depth, depth)
        return pltpu.make_async_copy(src.at[window], dst.at[window], load_sem.at[slot, part])

    q_loads = [load(wq_hbm, wq, 0, i) for i in range(parts)]
    o_loads = [load(wo_hbm, wo, 1, i) for i in range(parts)]
    own_x = pltpu.make_async_copy(tok, xg.at[me], own_sem)
    own_k = pltpu.make_async_copy(keys, kg.at[pl.ds(0, span)], kv_own.at[0])
    own_v = pltpu.make_async_copy(values, vg.at[pl.ds(0, span)], kv_own.at[1])

    barrier = pltpu.get_barrier_semaphore()
    for step in range(1, n):
        pl.semaphore_signal(
            barrier, inc=1, device_id={"tensor": lax.rem(me + step, n)}, device_id_type=MESH
        )
    for bit in bits:
        pl.semaphore_signal(
            barrier, inc=1, device_id={"frame": flip(me_f, bit)}, device_id_type=MESH
        )
    own_x.start()
    own_k.start()
    own_v.start()
    for copy in q_loads + o_loads:
        copy.start()
    pl.semaphore_wait(barrier, n - 1 + len(bits))

    def token_copy(block, side, source=None):
        towards = me + 1 if side == 0 else me - 1
        towards = lax.rem(towards + n, n)
        return pltpu.make_async_remote_copy(
            src_ref=xg.at[block] if source is None else source,
            dst_ref=xg.at[block],
            send_sem=x_send.at[side, block],
            recv_sem=x_recv.at[block],
            device_id={"tensor": towards},
            device_id_type=MESH,
        )

    @pl.when(me < n - 1)
    def _():
        token_copy(me, 0, tok).start()

    @pl.when(me > 0)
    def _():
        token_copy(me, 1, tok).start()

    def exchange(ref, source, send, recv, order, phase):
        bit = order[phase]
        held = [0]
        for earlier in order[:phase]:
            held = held + [slot + earlier for slot in held]
        copies = []
        for slot in held:
            src = source if slot == 0 else ref.at[pl.ds(slot * span, span)]
            copies.append(
                pltpu.make_async_remote_copy(
                    src_ref=src,
                    dst_ref=ref.at[pl.ds((slot + bit) * span, span)],
                    send_sem=send.at[slot + bit],
                    recv_sem=recv.at[slot + bit],
                    device_id={"frame": flip(me_f, bit)},
                    device_id_type=MESH,
                )
            )
        return copies

    phases = [
        exchange(kg, keys, k_send, k_recv, k_order, p)
        + exchange(vg, values, v_send, v_recv, v_order, p)
        for p in range(len(bits))
    ]

    def begin(p):
        for copy in phases[p]:
            copy.start()

    def finish(p):
        for copy in phases[p]:
            copy.wait_recv()

    begin(0)
    for p in range(1, len(bits)):
        finish(p - 1)
        begin(p)

    slot_of = lax.broadcasted_iota(jnp.int32, (1, span), 1)
    pieces = []
    for slot in range(frames_n):
        owner = me_f
        for bit in bits:
            if slot & bit:
                owner = flip(owner, bit)
        pieces.append(slot_of + owner * span)
    frame_index = jnp.concatenate(pieces, axis=1)
    visible_frames = frame_index < frames_n * span - pad[0]

    def part_copy(block, tile, slot=None):
        window = pl.ds(pl.multiple_of(tile * o_tile, o_tile), o_tile)
        return pltpu.make_async_remote_copy(
            src_ref=pbuf.at[block, :, window],
            dst_ref=rbuf.at[me if slot is None else slot, :, window],
            send_sem=p_send.at[block, tile],
            recv_sem=p_recv.at[me if slot is None else slot, tile],
            device_id={"tensor": block},
            device_id_type=MESH,
        )

    def process(block, first, mine):
        hidden = xg[block].astype(jnp.float32)
        factor = lax.rsqrt(jnp.mean(hidden * hidden, axis=-1, keepdims=True) + epsilon)
        nbuf[...] = (hidden * factor * gain[...]).astype(jnp.bfloat16)

        @pl.when(first)
        def _():
            for copy in q_loads:
                copy.wait()

        def q_body(tile, _):
            window = pl.ds(pl.multiple_of(tile * q_tile, q_tile), q_tile)
            q = jnp.dot(nbuf[...], wq[:, window], preferred_element_type=jnp.float32)
            qbuf[:, window] = (q * HEAD_DIM ** (-0.5)).astype(jnp.bfloat16)
            return 0

        lax.fori_loop(0, cols // q_tile, q_body, 0)

        @pl.when(first)
        def _():
            finish(len(bits) - 1)
            own_k.wait()
            own_v.wait()

        block_pos = pos[pl.ds(pl.multiple_of(block * rows, rows), rows), :]
        visible = (frame_index <= block_pos) & visible_frames
        for head in range(cols // HEAD_DIM):
            window = slice(head * HEAD_DIM, (head + 1) * HEAD_DIM)
            scores = lax.dot_general(
                qbuf[:, window], kg[:, window], (((1,), (1,)), ((), ())),
                preferred_element_type=jnp.float32,
            )
            scores = jnp.where(visible, scores, masked_score)
            highest = jnp.max(scores, axis=-1, keepdims=True)
            weights = jnp.where(visible, jnp.exp(scores - highest), 0.0)
            total = jnp.sum(weights, axis=-1, keepdims=True)
            mixed = jnp.dot(
                weights.astype(jnp.bfloat16), vg[:, window], preferred_element_type=jnp.float32
            )
            abuf[:, window] = (mixed / total).astype(jnp.bfloat16)

        @pl.when(first)
        def _():
            for copy in o_loads:
                copy.wait()

        def o_body(tile, _):
            window = pl.ds(pl.multiple_of(tile * o_tile, o_tile), o_tile)
            pbuf[block, :, window] = jnp.dot(
                abuf[...], wo[:, window], preferred_element_type=jnp.float32
            ).astype(jnp.bfloat16)

            @pl.when(jnp.logical_and(jnp.logical_not(mine), tile > 0))
            def _():
                part_copy(block, tile - 1).start()

            return 0

        lax.fori_loop(0, n_out, o_body, 0)

        @pl.when(jnp.logical_not(mine))
        def _():
            part_copy(block, n_out - 1).start()

    def round_body(index, _):
        stage = lax.div(index, 2) + 1
        side = lax.rem(index, 2)
        before = me - stage
        after = me + stage

        @pl.when(jnp.logical_and(side == 0, before >= 0))
        def _():
            token_copy(before, 0).wait_recv()

            @pl.when(me < n - 1)
            def _():
                token_copy(before, 0).start()

        @pl.when(jnp.logical_and(side == 0, after < n))
        def _():
            token_copy(after, 1).wait_recv()

            @pl.when(me > 0)
            def _():
                token_copy(after, 1).start()

        mine = index == 2 * (n - 1)

        @pl.when(mine)
        def _():
            own_x.wait()

        block = jnp.where(mine, me, jnp.where(side == 0, before, after))
        first = jnp.logical_or(index == 0, jnp.logical_and(index == 1, me == 0))

        @pl.when(jnp.logical_and(block >= 0, block < n))
        def _():
            process(block, first, mine)

        return 0

    lax.fori_loop(0, 2 * (n - 1) + 1, round_body, 0)

    def sum_body(tile, _):
        window = pl.ds(pl.multiple_of(tile * o_tile, o_tile), o_tile)
        total = pbuf[me, :, window].astype(jnp.float32)
        for step in range(1, n):
            peer = lax.rem(me + step, n)
            part_copy(peer, tile, peer).wait_recv()
            total = total + rbuf[peer, :, window].astype(jnp.float32)
        out[:, window] = total.astype(jnp.bfloat16)
        return 0

    lax.fori_loop(0, n_out, sum_body, 0)

    def drain_body(step, _):
        peer = lax.rem(me + step, n)
        for tile in range(n_out):
            part_copy(peer, tile).wait_send()
        return 0

    lax.fori_loop(1, n, drain_body, 0)

    def drain_tokens(block, _):
        @pl.when(jnp.logical_and(me < n - 1, block <= me))
        def _():
            token_copy(block, 0).wait_send()

        @pl.when(jnp.logical_and(me > 0, block >= me))
        def _():
            token_copy(block, 1).wait_send()

        return 0

    lax.fori_loop(0, n, drain_tokens, 0)
    for group in phases:
        for copy in group:
            copy.wait_send()


def divisor(total, most):
    return math.gcd(total, most)


def per_device(
    n, frames_n,
    tokens, norm_gain, query_weight, out_weight, cache_keys, cache_values, token_pos, frame_pad
):
    rows, seqs, width = tokens.shape
    cols = query_weight.shape[1]
    span = cache_keys.shape[0]
    q_tile = divisor(cols, 512)
    o_tile = divisor(width, 1024)
    parts = 4
    n_out = width // o_tile
    hbm = pl.BlockSpec(memory_space=pl.ANY)
    vmem = pl.BlockSpec(memory_space=pltpu.VMEM)
    bf16 = jnp.bfloat16
    dma = pltpu.SemaphoreType.DMA
    result = pl.pallas_call(
        functools.partial(kernel, n, frames_n, q_tile, o_tile, parts),
        out_shape=jax.ShapeDtypeStruct((rows, width), bf16),
        in_specs=[hbm, vmem, hbm, hbm, hbm, hbm, vmem, pl.BlockSpec(memory_space=pltpu.SMEM)],
        out_specs=vmem,
        scratch_shapes=[
            pltpu.VMEM(query_weight.shape, bf16),
            pltpu.VMEM(out_weight.shape, bf16),
            pltpu.VMEM((frames_n * span, cols), bf16),
            pltpu.VMEM((frames_n * span, cols), bf16),
            pltpu.VMEM((n, rows, width), bf16),
            pltpu.VMEM((rows, width), bf16),
            pltpu.VMEM((rows, cols), bf16),
            pltpu.VMEM((rows, cols), bf16),
            pltpu.VMEM((n, rows, width), bf16),
            pltpu.VMEM((n, rows, width), bf16),
            dma((2, parts)),
            dma(()),
            dma((2,)),
            dma((frames_n,)),
            dma((frames_n,)),
            dma((frames_n,)),
            dma((frames_n,)),
            dma((2, n)),
            dma((n,)),
            dma((n, n_out)),
            dma((n, n_out)),
        ],
        compiler_params=pltpu.CompilerParams(collective_id=0, has_side_effects=True),
    )(
        tokens.reshape(rows, width),
        norm_gain.reshape(1, width),
        query_weight,
        out_weight,
        cache_keys.reshape(span, cols),
        cache_values.reshape(span, cols),
        token_pos,
        frame_pad,
    )
    return result.reshape(rows, seqs, width)


def solution(mesh):
    placed = (
        P(("frame", "tensor"), None, None),
        P(),
        P(None, "tensor"),
        P("tensor", None),
        P("frame", None, "tensor"),
        P("frame", None, "tensor"),
        P("frame", None),
        P(),
    )
    return jax.shard_map(
        functools.partial(per_device, mesh.shape["tensor"], mesh.shape["frame"]),
        mesh=mesh,
        in_specs=placed,
        out_specs=P(("frame", "tensor"), None, None),
        check_vma=False,
    )
```

```python
import functools
import math

import jax
import jax.numpy as jnp
from jax import lax
from jax.experimental import pallas as pl
from jax.experimental.pallas import tpu as pltpu
from jax.sharding import PartitionSpec as P

HEAD_DIM = 128
epsilon = 1e-06
masked_score = -1e30
MESH = pl.DeviceIdType.MESH


def flip(index, bit):
    return index + bit - 2 * bit * lax.rem(lax.div(index, bit), 2)


def kernel(
    n, frames_n, x_tile, o_tile,
    tok, gain, wq_hbm, wo_hbm, keys, values, pos, pad,
    out,
    wq, wo, kg, vg, raw, xg, qacc, qall, abuf, pbuf, rbuf,
    q_sem, o_sem, own_sem, kv_own, k_send, k_recv, v_send, v_recv,
    x_send, x_recv, p_send, p_recv,
):
    me_f = lax.axis_index("frame")
    me = lax.axis_index("tensor")
    rows = tok.shape[0]
    width = tok.shape[1]
    cols = wq.shape[1]
    span = keys.shape[0]
    bits = [1 << b for b in range(int(math.log2(frames_n)))][::-1]
    phase_n = len(bits)
    v_order = bits[1::-1] + bits[2:] if phase_n > 1 else bits
    n_x = width // x_tile
    n_out = width // o_tile
    has_left = me > 0
    has_right = me < n - 1
    middle = jnp.logical_and(has_left, has_right)
    low_half = 2 * me < n

    def q_load(part):
        window = pl.ds(pl.multiple_of(part * x_tile, x_tile), x_tile)
        return pltpu.make_async_copy(wq_hbm.at[window], wq.at[window], q_sem.at[part])

    def o_load(part):
        depth = cols // 2
        window = pl.ds(part * depth, depth)
        return pltpu.make_async_copy(wo_hbm.at[window], wo.at[window], o_sem.at[part])

    own_x = pltpu.make_async_copy(tok, raw, own_sem)
    own_k = pltpu.make_async_copy(keys, kg.at[pl.ds(0, span)], kv_own.at[0])
    own_v = pltpu.make_async_copy(values, vg.at[pl.ds(0, span)], kv_own.at[1])

    own_x.start()
    barrier = pltpu.get_barrier_semaphore()
    for bit in bits:
        pl.semaphore_signal(
            barrier, inc=1, device_id={"frame": flip(me_f, bit)}, device_id_type=MESH
        )

    @pl.when(has_left)
    def _():
        pl.semaphore_signal(barrier, inc=1, device_id={"tensor": me - 1}, device_id_type=MESH)

    @pl.when(has_right)
    def _():
        pl.semaphore_signal(barrier, inc=1, device_id={"tensor": me + 1}, device_id_type=MESH)

    own_k.start()
    own_v.start()
    for part in range(n_x):
        q_load(part).start()
    for part in range(2):
        o_load(part).start()

    own_x.wait()
    hidden = raw[...].astype(jnp.float32)
    factor = lax.rsqrt(jnp.mean(hidden * hidden, axis=-1, keepdims=True) + epsilon)
    xg[me] = (hidden * factor * gain[...]).astype(jnp.bfloat16)

    pl.semaphore_wait(barrier, phase_n + jnp.minimum(me, 1) + jnp.minimum(n - 1 - me, 1))

    def token_copy(block, side, chunk):
        towards = lax.rem(me + 1 - 2 * side + n, n)
        window = pl.ds(pl.multiple_of(chunk * x_tile, x_tile), x_tile)
        return pltpu.make_async_remote_copy(
            src_ref=xg.at[block, :, window],
            dst_ref=xg.at[block, :, window],
            send_sem=x_send.at[side, block, chunk],
            recv_sem=x_recv.at[block, chunk],
            device_id={"tensor": towards},
            device_id_type=MESH,
        )

    for chunk in range(n_x):
        @pl.when(has_right)
        def _():
            token_copy(me, 0, chunk).start()

        @pl.when(has_left)
        def _():
            token_copy(me, 1, chunk).start()

    def exchange(ref, source, send, recv, order, phase):
        bit = order[phase]
        held = [0]
        for earlier in order[:phase]:
            held = held + [slot + earlier for slot in held]
        copies = []
        for slot in held:
            src = source if slot == 0 else ref.at[pl.ds(slot * span, span)]
            copies.append(
                pltpu.make_async_remote_copy(
                    src_ref=src,
                    dst_ref=ref.at[pl.ds((slot + bit) * span, span)],
                    send_sem=send.at[slot + bit],
                    recv_sem=recv.at[slot + bit],
                    device_id={"frame": flip(me_f, bit)},
                    device_id_type=MESH,
                )
            )
        return copies

    phases = [
        exchange(kg, keys, k_send, k_recv, bits, p)
        + exchange(vg, values, v_send, v_recv, v_order, p)
        for p in range(phase_n)
    ]

    def begin(p):
        for copy in phases[p]:
            copy.start()

    def finish(p):
        for copy in phases[p]:
            copy.wait_recv()

    begin(0)

    slot_of = lax.broadcasted_iota(jnp.int32, (1, span), 1)
    pieces = []
    for slot in range(frames_n):
        owner = me_f
        for bit in bits:
            if slot & bit:
                owner = flip(owner, bit)
        pieces.append(slot_of + owner * span)
    frame_index = jnp.concatenate(pieces, axis=1)
    visible_frames = frame_index < frames_n * span - pad[0]

    def q_step(block, side, chunk):
        window = pl.ds(pl.multiple_of(chunk * x_tile, x_tile), x_tile)
        product = jnp.dot(xg[block, :, window], wq[window, :], preferred_element_type=jnp.float32)

        @pl.when(chunk == 0)
        def _():
            qacc[side] = product

        @pl.when(chunk > 0)
        def _():
            qacc[side] += product

        @pl.when(chunk == n_x - 1)
        def _():
            qall[block] = (qacc[side] * HEAD_DIM ** (-0.5)).astype(jnp.bfloat16)

    def own_body(chunk, _):
        q_load(chunk).wait()
        q_step(me, 0, chunk)
        return 0

    lax.fori_loop(0, n_x, own_body, 0)
    for p in range(1, phase_n - 1):
        finish(p - 1)
        begin(p)

    def part_copy(block, side, tile):
        towards = lax.rem(me + 1 - 2 * side + n, n)
        window = pl.ds(pl.multiple_of(tile * o_tile, o_tile), o_tile)
        return pltpu.make_async_remote_copy(
            src_ref=pbuf.at[block, :, window],
            dst_ref=rbuf.at[side, block, :, window],
            send_sem=p_send.at[block, tile],
            recv_sem=p_recv.at[side, block, tile],
            device_id={"tensor": towards},
            device_id_type=MESH,
        )

    def attend(block, send, side):
        block_pos = pos[pl.ds(pl.multiple_of(block * rows, rows), rows), :]
        visible = (frame_index <= block_pos) & visible_frames
        for head in range(cols // HEAD_DIM):
            window = slice(head * HEAD_DIM, (head + 1) * HEAD_DIM)
            scores = lax.dot_general(
                qall[block, :, window], kg[:, window], (((1,), (1,)), ((), ())),
                preferred_element_type=jnp.float32,
            )
            scores = jnp.where(visible, scores, masked_score)
            highest = jnp.max(scores, axis=-1, keepdims=True)
            weights = jnp.where(visible, jnp.exp(scores - highest), 0.0)
            total = jnp.sum(weights, axis=-1, keepdims=True)
            mixed = jnp.dot(
                weights.astype(jnp.bfloat16), vg[:, window], preferred_element_type=jnp.float32
            )
            abuf[:, window] = (mixed / total).astype(jnp.bfloat16)

        def o_body(tile, _):
            window = pl.ds(pl.multiple_of(tile * o_tile, o_tile), o_tile)
            pbuf[block, :, window] = jnp.dot(
                abuf[...], wo[:, window], preferred_element_type=jnp.float32
            ).astype(jnp.bfloat16)
            if send:
                @pl.when(tile > 0)
                def _():
                    part_copy(block, side, tile - 1).start()
            return 0

        lax.fori_loop(0, n_out, o_body, 0)
        if send:
            part_copy(block, side, n_out - 1).start()

    def stage_body(stage, _):
        before = me - stage
        after = me + stage

        def chunk_body(chunk, _):
            @pl.when(before >= 0)
            def _():
                token_copy(before, 0, chunk).wait_recv()

                @pl.when(has_right)
                def _():
                    token_copy(before, 0, chunk).start()

            @pl.when(after < n)
            def _():
                token_copy(after, 1, chunk).wait_recv()

                @pl.when(has_left)
                def _():
                    token_copy(after, 1, chunk).start()

            def side_body(side, _):
                block = me + (2 * side - 1) * stage

                @pl.when(jnp.logical_and(block >= 0, block < n))
                def _():
                    q_step(block, side, chunk)

                return 0

            lax.fori_loop(0, 2, side_body, 0)
            return 0

        lax.fori_loop(0, n_x, chunk_body, 0)

        @pl.when(stage == 1)
        def _():
            if phase_n > 1:
                finish(phase_n - 2)
                begin(phase_n - 1)
            finish(phase_n - 1)
            own_k.wait()
            own_v.wait()
            for part in range(2):
                o_load(part).wait()

        @pl.when(jnp.logical_not(middle))
        def _():
            attend(
                jnp.where(has_left, n - 1 - stage, stage), True, jnp.where(has_left, 1, 0)
            )

        return 0

    lax.fori_loop(1, n, stage_body, 0)

    def late_body(index, _):
        step = jnp.where(low_half, index, n - index)
        block = lax.rem(me + step, n)

        @pl.when(jnp.logical_or(middle, index == n))
        def _():
            attend(block, False, 0)

        return 0

    lax.fori_loop(1, n + 1, late_body, 0)

    def relay_body(index, _):
        stage = lax.div(index, n_out)
        tile = lax.rem(index, n_out)
        window = pl.ds(pl.multiple_of(tile * o_tile, o_tile), o_tile)

        def side_body(turn, _):
            side = jnp.where(low_half, turn, 1 - turn)
            block = jnp.where(side == 0, stage, n - 1 - stage)
            passes = jnp.where(side == 0, block > me, block < me)

            @pl.when(jnp.logical_and(middle, passes))
            def _():
                part_copy(block, side, tile).wait_recv()
                pbuf[block, :, window] = (
                    pbuf[block, :, window].astype(jnp.float32)
                    + rbuf[side, block, :, window].astype(jnp.float32)
                ).astype(jnp.bfloat16)
                part_copy(block, side, tile).start()

            return 0

        lax.fori_loop(0, 2, side_body, 0)
        return 0

    lax.fori_loop(n_out, n * n_out, relay_body, 0)

    def sum_body(tile, _):
        window = pl.ds(pl.multiple_of(tile * o_tile, o_tile), o_tile)

        @pl.when(has_left)
        def _():
            part_copy(me, 0, tile).wait_recv()

        @pl.when(has_right)
        def _():
            part_copy(me, 1, tile).wait_recv()

        total = pbuf[me, :, window].astype(jnp.float32)
        zero = jnp.zeros_like(total)
        total = total + jnp.where(has_left, rbuf[0, me, :, window].astype(jnp.float32), zero)
        total = total + jnp.where(has_right, rbuf[1, me, :, window].astype(jnp.float32), zero)
        out[:, window] = total.astype(jnp.bfloat16)
        return 0

    lax.fori_loop(0, n_out, sum_body, 0)

    def drain_body(block, _):
        for tile in range(n_out):
            @pl.when(block != me)
            def _():
                part_copy(block, 0, tile).wait_send()

        for chunk in range(n_x):
            @pl.when(jnp.logical_and(has_right, block <= me))
            def _():
                token_copy(block, 0, chunk).wait_send()

            @pl.when(jnp.logical_and(has_left, block >= me))
            def _():
                token_copy(block, 1, chunk).wait_send()

        return 0

    lax.fori_loop(0, n, drain_body, 0)
    for group in phases:
        for copy in group:
            copy.wait_send()


def divisor(total, most):
    return math.gcd(total, most)


def per_device(
    n, frames_n,
    tokens, norm_gain, query_weight, out_weight, cache_keys, cache_values, token_pos, frame_pad
):
    rows, seqs, width = tokens.shape
    cols = query_weight.shape[1]
    span = cache_keys.shape[0]
    x_tile = divisor(width, 1024)
    o_tile = divisor(width, 1024)
    n_x = width // x_tile
    n_out = width // o_tile
    hbm = pl.BlockSpec(memory_space=pl.ANY)
    vmem = pl.BlockSpec(memory_space=pltpu.VMEM)
    bf16 = jnp.bfloat16
    dma = pltpu.SemaphoreType.DMA
    result = pl.pallas_call(
        functools.partial(kernel, n, frames_n, x_tile, o_tile),
        out_shape=jax.ShapeDtypeStruct((rows, width), bf16),
        in_specs=[hbm, vmem, hbm, hbm, hbm, hbm, vmem, pl.BlockSpec(memory_space=pltpu.SMEM)],
        out_specs=vmem,
        scratch_shapes=[
            pltpu.VMEM(query_weight.shape, bf16),
            pltpu.VMEM(out_weight.shape, bf16),
            pltpu.VMEM((frames_n * span, cols), bf16),
            pltpu.VMEM((frames_n * span, cols), bf16),
            pltpu.VMEM((rows, width), bf16),
            pltpu.VMEM((n, rows, width), bf16),
            pltpu.VMEM((2, rows, cols), jnp.float32),
            pltpu.VMEM((n, rows, cols), bf16),
            pltpu.VMEM((rows, cols), bf16),
            pltpu.VMEM((n, rows, width), bf16),
            pltpu.VMEM((2, n, rows, width), bf16),
            dma((n_x,)),
            dma((2,)),
            dma(()),
            dma((2,)),
            dma((frames_n,)),
            dma((frames_n,)),
            dma((frames_n,)),
            dma((frames_n,)),
            dma((2, n, n_x)),
            dma((n, n_x)),
            dma((n, n_out)),
            dma((2, n, n_out)),
        ],
        compiler_params=pltpu.CompilerParams(collective_id=0, has_side_effects=True),
    )(
        tokens.reshape(rows, width),
        norm_gain.reshape(1, width),
        query_weight,
        out_weight,
        cache_keys.reshape(span, cols),
        cache_values.reshape(span, cols),
        token_pos,
        frame_pad,
    )
    return result.reshape(rows, seqs, width)


def solution(mesh):
    placed = (
        P(("frame", "tensor"), None, None),
        P(),
        P(None, "tensor"),
        P("tensor", None),
        P("frame", None, "tensor"),
        P("frame", None, "tensor"),
        P("frame", None),
        P(),
    )
    return jax.shard_map(
        functools.partial(per_device, mesh.shape["tensor"], mesh.shape["frame"]),
        mesh=mesh,
        in_specs=placed,
        out_specs=P(("frame", "tensor"), None, None),
        check_vma=False,
    )
```

```python
import functools
import math

import jax
import jax.numpy as jnp
from jax import lax
from jax.experimental import pallas as pl
from jax.experimental.pallas import tpu as pltpu
from jax.sharding import PartitionSpec as P

HEAD_DIM = 128
epsilon = 1e-06
masked_score = -1e30
MESH = pl.DeviceIdType.MESH


def flip(index, bit):
    return index + bit - 2 * bit * lax.rem(lax.div(index, bit), 2)


def kernel(
    n, frames_n, x_tile, o_tile,
    tok, gain, wq_hbm, wo_hbm, keys, values, pos, pad,
    out,
    wq, wo, kg, vg, raw, xg, qacc, qall, abuf, pbuf, rbuf,
    q_sem, o_sem, own_sem, kv_own, k_send, k_recv, v_send, v_recv,
    x_send, x_recv, p_send, p_recv,
):
    me_f = lax.axis_index("frame")
    me = lax.axis_index("tensor")
    rows = tok.shape[0]
    width = tok.shape[1]
    cols = wq.shape[1]
    span = keys.shape[0]
    bits = [1 << b for b in range(int(math.log2(frames_n)))][::-1]
    phase_n = len(bits)
    v_order = bits[1::-1] + bits[2:] if phase_n > 1 else bits
    n_x = width // x_tile
    n_out = width // o_tile
    lag = n_out // 2
    has_left = me > 0
    has_right = me < n - 1
    middle = jnp.logical_and(has_left, has_right)
    low_half = 2 * me < n

    def q_load(part):
        window = pl.ds(pl.multiple_of(part * x_tile, x_tile), x_tile)
        return pltpu.make_async_copy(wq_hbm.at[window], wq.at[window], q_sem.at[part])

    def o_load(part):
        depth = cols // 2
        window = pl.ds(part * depth, depth)
        return pltpu.make_async_copy(wo_hbm.at[window], wo.at[window], o_sem.at[part])

    own_x = pltpu.make_async_copy(tok, raw, own_sem)
    own_k = pltpu.make_async_copy(keys, kg.at[pl.ds(0, span)], kv_own.at[0])
    own_v = pltpu.make_async_copy(values, vg.at[pl.ds(0, span)], kv_own.at[1])

    own_x.start()
    barrier = pltpu.get_barrier_semaphore()
    for bit in bits:
        pl.semaphore_signal(
            barrier, inc=1, device_id={"frame": flip(me_f, bit)}, device_id_type=MESH
        )

    @pl.when(has_left)
    def _():
        pl.semaphore_signal(barrier, inc=1, device_id={"tensor": me - 1}, device_id_type=MESH)

    @pl.when(has_right)
    def _():
        pl.semaphore_signal(barrier, inc=1, device_id={"tensor": me + 1}, device_id_type=MESH)

    own_k.start()
    own_v.start()
    for part in range(n_x):
        q_load(part).start()
    for part in range(2):
        o_load(part).start()

    own_x.wait()
    hidden = raw[...].astype(jnp.float32)
    factor = lax.rsqrt(jnp.mean(hidden * hidden, axis=-1, keepdims=True) + epsilon)
    xg[me] = (hidden * factor * gain[...]).astype(jnp.bfloat16)

    pl.semaphore_wait(barrier, phase_n + jnp.minimum(me, 1) + jnp.minimum(n - 1 - me, 1))

    def token_copy(block, side, chunk):
        towards = lax.rem(me + 1 - 2 * side + n, n)
        window = pl.ds(pl.multiple_of(chunk * x_tile, x_tile), x_tile)
        return pltpu.make_async_remote_copy(
            src_ref=xg.at[block, :, window],
            dst_ref=xg.at[block, :, window],
            send_sem=x_send.at[side, block, chunk],
            recv_sem=x_recv.at[block, chunk],
            device_id={"tensor": towards},
            device_id_type=MESH,
        )

    for chunk in range(n_x):
        @pl.when(has_right)
        def _():
            token_copy(me, 0, chunk).start()

        @pl.when(has_left)
        def _():
            token_copy(me, 1, chunk).start()

    def exchange(ref, source, send, recv, order, phase):
        bit = order[phase]
        held = [0]
        for earlier in order[:phase]:
            held = held + [slot + earlier for slot in held]
        copies = []
        for slot in held:
            src = source if slot == 0 else ref.at[pl.ds(slot * span, span)]
            copies.append(
                pltpu.make_async_remote_copy(
                    src_ref=src,
                    dst_ref=ref.at[pl.ds((slot + bit) * span, span)],
                    send_sem=send.at[slot + bit],
                    recv_sem=recv.at[slot + bit],
                    device_id={"frame": flip(me_f, bit)},
                    device_id_type=MESH,
                )
            )
        return copies

    phases = [
        exchange(kg, keys, k_send, k_recv, bits, p)
        + exchange(vg, values, v_send, v_recv, v_order, p)
        for p in range(phase_n)
    ]

    def begin(p):
        for copy in phases[p]:
            copy.start()

    def finish(p):
        for copy in phases[p]:
            copy.wait_recv()

    begin(0)

    slot_of = lax.broadcasted_iota(jnp.int32, (1, span), 1)
    pieces = []
    for slot in range(frames_n):
        owner = me_f
        for bit in bits:
            if slot & bit:
                owner = flip(owner, bit)
        pieces.append(slot_of + owner * span)
    frame_index = jnp.concatenate(pieces, axis=1)
    visible_frames = frame_index < frames_n * span - pad[0]

    def q_step(block, side, chunk):
        window = pl.ds(pl.multiple_of(chunk * x_tile, x_tile), x_tile)
        product = jnp.dot(xg[block, :, window], wq[window, :], preferred_element_type=jnp.float32)

        @pl.when(chunk == 0)
        def _():
            qacc[side] = product

        @pl.when(chunk > 0)
        def _():
            qacc[side] += product

        @pl.when(chunk == n_x - 1)
        def _():
            qall[block] = (qacc[side] * HEAD_DIM ** (-0.5)).astype(jnp.bfloat16)

    def own_body(chunk, _):
        q_load(chunk).wait()
        q_step(me, 0, chunk)
        return 0

    lax.fori_loop(0, n_x, own_body, 0)
    for p in range(1, phase_n - 1):
        finish(p - 1)
        begin(p)

    def part_copy(block, side, tile):
        towards = lax.rem(me + 1 - 2 * side + n, n)
        window = pl.ds(pl.multiple_of(tile * o_tile, o_tile), o_tile)
        return pltpu.make_async_remote_copy(
            src_ref=pbuf.at[block, :, window],
            dst_ref=rbuf.at[side, block, :, window],
            send_sem=p_send.at[block, tile],
            recv_sem=p_recv.at[side, block, tile],
            device_id={"tensor": towards},
            device_id_type=MESH,
        )

    def attend(block, send, side):
        block_pos = pos[pl.ds(pl.multiple_of(block * rows, rows), rows), :]
        visible = (frame_index <= block_pos) & visible_frames
        windows = [slice(i, i + HEAD_DIM) for i in range(0, cols, HEAD_DIM)]
        scores = [
            lax.dot_general(
                qall[block, :, window], kg[:, window], (((1,), (1,)), ((), ())),
                preferred_element_type=jnp.float32,
            )
            for window in windows
        ]
        scores = [jnp.where(visible, score, masked_score) for score in scores]
        highest = [jnp.max(score, axis=-1, keepdims=True) for score in scores]
        weights = [
            jnp.where(visible, jnp.exp(score - top), 0.0) for score, top in zip(scores, highest)
        ]
        totals = [jnp.sum(weight, axis=-1, keepdims=True) for weight in weights]
        gathered = [
            jnp.dot(weight.astype(jnp.bfloat16), vg[:, window], preferred_element_type=jnp.float32)
            for weight, window in zip(weights, windows)
        ]
        for window, value, total in zip(windows, gathered, totals):
            abuf[:, window] = (value / total).astype(jnp.bfloat16)

        def o_body(tile, _):
            window = pl.ds(pl.multiple_of(tile * o_tile, o_tile), o_tile)
            pbuf[block, :, window] = jnp.dot(
                abuf[...], wo[:, window], preferred_element_type=jnp.float32
            ).astype(jnp.bfloat16)
            if send is not False:
                @pl.when(jnp.logical_and(send, tile > 0))
                def _():
                    part_copy(block, side, tile - 1).start()
            return 0

        lax.fori_loop(0, n_out, o_body, 0)
        if send is not False:
            @pl.when(send)
            def _():
                part_copy(block, side, n_out - 1).start()

    def stage_body(stage, _):
        before = me - stage
        after = me + stage

        def chunk_body(chunk, _):
            @pl.when(before >= 0)
            def _():
                token_copy(before, 0, chunk).wait_recv()

                @pl.when(has_right)
                def _():
                    token_copy(before, 0, chunk).start()

            @pl.when(after < n)
            def _():
                token_copy(after, 1, chunk).wait_recv()

                @pl.when(has_left)
                def _():
                    token_copy(after, 1, chunk).start()

            def side_body(side, _):
                block = me + (2 * side - 1) * stage

                @pl.when(jnp.logical_and(block >= 0, block < n))
                def _():
                    q_step(block, side, chunk)

                return 0

            lax.fori_loop(0, 2, side_body, 0)
            return 0

        lax.fori_loop(0, n_x, chunk_body, 0)

        @pl.when(stage == 1)
        def _():
            if phase_n > 1:
                finish(phase_n - 2)
                begin(phase_n - 1)
            finish(phase_n - 1)
            own_k.wait()
            own_v.wait()
            for part in range(2):
                o_load(part).wait()

        @pl.when(jnp.logical_or(jnp.logical_not(middle), stage == 1))
        def _():
            end_block = jnp.where(has_left, n - 1 - stage, stage)
            near_block = jnp.where(low_half, me + 1, me - 1)
            attend(
                jnp.where(middle, near_block, end_block),
                jnp.logical_not(middle),
                jnp.where(has_left, 1, 0),
            )

        return 0

    lax.fori_loop(1, n, stage_body, 0)

    def relay_body(index, _):
        def side_body(turn, _):
            side = jnp.where(low_half, turn, 1 - turn)
            at = index - turn * lag
            stage = lax.div(at, n_out)
            tile = lax.rem(at, n_out)
            window = pl.ds(pl.multiple_of(tile * o_tile, o_tile), o_tile)
            block = jnp.where(side == 0, stage, n - 1 - stage)
            passes = jnp.where(side == 0, block > me, block < me)
            known = jnp.logical_and(at >= n_out, at < n * n_out)

            @pl.when(jnp.logical_and(known, passes))
            def _():
                part_copy(block, side, tile).wait_recv()
                pbuf[block, :, window] = (
                    pbuf[block, :, window].astype(jnp.float32)
                    + rbuf[side, block, :, window].astype(jnp.float32)
                ).astype(jnp.bfloat16)
                part_copy(block, side, tile).start()

            return 0

        lax.fori_loop(0, 2, side_body, 0)
        return 0

    def late_body(index, _):
        step = jnp.where(low_half, index, n - index)
        block = lax.rem(me + step, n)

        @pl.when(jnp.logical_and(middle, index == n))
        def _():
            lax.fori_loop(n_out, n * n_out + lag, relay_body, 0)

        @pl.when(jnp.logical_or(middle, index == n))
        def _():
            attend(block, False, 0)

        return 0

    lax.fori_loop(2, n + 1, late_body, 0)

    def sum_body(tile, _):
        window = pl.ds(pl.multiple_of(tile * o_tile, o_tile), o_tile)

        @pl.when(has_left)
        def _():
            part_copy(me, 0, tile).wait_recv()

        @pl.when(has_right)
        def _():
            part_copy(me, 1, tile).wait_recv()

        total = pbuf[me, :, window].astype(jnp.float32)
        zero = jnp.zeros_like(total)
        total = total + jnp.where(has_left, rbuf[0, me, :, window].astype(jnp.float32), zero)
        total = total + jnp.where(has_right, rbuf[1, me, :, window].astype(jnp.float32), zero)
        out[:, window] = total.astype(jnp.bfloat16)
        return 0

    lax.fori_loop(0, n_out, sum_body, 0)

    def drain_body(block, _):
        for tile in range(n_out):
            @pl.when(block != me)
            def _():
                part_copy(block, 0, tile).wait_send()

        for chunk in range(n_x):
            @pl.when(jnp.logical_and(has_right, block <= me))
            def _():
                token_copy(block, 0, chunk).wait_send()

            @pl.when(jnp.logical_and(has_left, block >= me))
            def _():
                token_copy(block, 1, chunk).wait_send()

        return 0

    lax.fori_loop(0, n, drain_body, 0)
    for group in phases:
        for copy in group:
            copy.wait_send()


def divisor(total, most):
    return math.gcd(total, most)


def per_device(
    n, frames_n,
    tokens, norm_gain, query_weight, out_weight, cache_keys, cache_values, token_pos, frame_pad
):
    rows, seqs, width = tokens.shape
    cols = query_weight.shape[1]
    span = cache_keys.shape[0]
    x_tile = divisor(width, 1024)
    o_tile = divisor(width, 512)
    n_x = width // x_tile
    n_out = width // o_tile
    hbm = pl.BlockSpec(memory_space=pl.ANY)
    vmem = pl.BlockSpec(memory_space=pltpu.VMEM)
    bf16 = jnp.bfloat16
    dma = pltpu.SemaphoreType.DMA
    result = pl.pallas_call(
        functools.partial(kernel, n, frames_n, x_tile, o_tile),
        out_shape=jax.ShapeDtypeStruct((rows, width), bf16),
        in_specs=[hbm, vmem, hbm, hbm, hbm, hbm, vmem, pl.BlockSpec(memory_space=pltpu.SMEM)],
        out_specs=vmem,
        scratch_shapes=[
            pltpu.VMEM(query_weight.shape, bf16),
            pltpu.VMEM(out_weight.shape, bf16),
            pltpu.VMEM((frames_n * span, cols), bf16),
            pltpu.VMEM((frames_n * span, cols), bf16),
            pltpu.VMEM((rows, width), bf16),
            pltpu.VMEM((n, rows, width), bf16),
            pltpu.VMEM((2, rows, cols), jnp.float32),
            pltpu.VMEM((n, rows, cols), bf16),
            pltpu.VMEM((rows, cols), bf16),
            pltpu.VMEM((n, rows, width), bf16),
            pltpu.VMEM((2, n, rows, width), bf16),
            dma((n_x,)),
            dma((2,)),
            dma(()),
            dma((2,)),
            dma((frames_n,)),
            dma((frames_n,)),
            dma((frames_n,)),
            dma((frames_n,)),
            dma((2, n, n_x)),
            dma((n, n_x)),
            dma((n, n_out)),
            dma((2, n, n_out)),
        ],
        compiler_params=pltpu.CompilerParams(collective_id=0, has_side_effects=True),
    )(
        tokens.reshape(rows, width),
        norm_gain.reshape(1, width),
        query_weight,
        out_weight,
        cache_keys.reshape(span, cols),
        cache_values.reshape(span, cols),
        token_pos,
        frame_pad,
    )
    return result.reshape(rows, seqs, width)


def solution(mesh):
    placed = (
        P(("frame", "tensor"), None, None),
        P(),
        P(None, "tensor"),
        P("tensor", None),
        P("frame", None, "tensor"),
        P("frame", None, "tensor"),
        P("frame", None),
        P(),
    )
    return jax.shard_map(
        functools.partial(per_device, mesh.shape["tensor"], mesh.shape["frame"]),
        mesh=mesh,
        in_specs=placed,
        out_specs=P(("frame", "tensor"), None, None),
        check_vma=False,
    )
```

```python
import functools
import math

import jax
import jax.numpy as jnp
from jax import lax
from jax.experimental import pallas as pl
from jax.experimental.pallas import tpu as pltpu
from jax.sharding import PartitionSpec as P

HEAD_DIM = 128
epsilon = 1e-06
masked_score = -1e30
MESH = pl.DeviceIdType.MESH


def flip(index, bit):
    return index + bit - 2 * bit * lax.rem(lax.div(index, bit), 2)


def kernel(
    n, frames_n, x_tile, o_tile,
    tok, gain, wq_hbm, wo_hbm, keys, values, pos, pad,
    out,
    wq, wo, kg, vg, raw, xg, qacc, qall, abuf, pbuf, rbuf,
    q_sem, o_sem, own_sem, kv_own, k_send, k_recv, v_send, v_recv,
    x_send, x_recv, p_send, p_recv,
):
    me_f = lax.axis_index("frame")
    me = lax.axis_index("tensor")
    rows = tok.shape[0]
    width = tok.shape[1]
    cols = wq.shape[1]
    span = keys.shape[0]
    bits = [1 << b for b in range(int(math.log2(frames_n)))][::-1]
    phase_n = len(bits)
    v_order = bits[1::-1] + bits[2:] if phase_n > 1 else bits
    n_x = width // x_tile
    n_out = width // o_tile
    lag = n_out // 2
    has_left = me > 0
    has_right = me < n - 1
    middle = jnp.logical_and(has_left, has_right)
    low_half = 2 * me < n

    def q_load(part):
        window = pl.ds(pl.multiple_of(part * x_tile, x_tile), x_tile)
        return pltpu.make_async_copy(wq_hbm.at[window], wq.at[window], q_sem.at[part])

    def o_load(part):
        depth = cols // 2
        window = pl.ds(part * depth, depth)
        return pltpu.make_async_copy(wo_hbm.at[window], wo.at[window], o_sem.at[part])

    own_x = pltpu.make_async_copy(tok, raw, own_sem)
    own_k = pltpu.make_async_copy(keys, kg.at[pl.ds(0, span)], kv_own.at[0])
    own_v = pltpu.make_async_copy(values, vg.at[pl.ds(0, span)], kv_own.at[1])

    own_x.start()
    barrier = pltpu.get_barrier_semaphore()
    for bit in bits:
        pl.semaphore_signal(
            barrier, inc=1, device_id={"frame": flip(me_f, bit)}, device_id_type=MESH
        )

    @pl.when(has_left)
    def _():
        pl.semaphore_signal(barrier, inc=1, device_id={"tensor": me - 1}, device_id_type=MESH)

    @pl.when(has_right)
    def _():
        pl.semaphore_signal(barrier, inc=1, device_id={"tensor": me + 1}, device_id_type=MESH)

    @pl.when(jnp.logical_not(middle))
    def _():
        pl.semaphore_signal(
            barrier, inc=1, device_id={"tensor": n - 1 - me}, device_id_type=MESH
        )

    own_k.start()
    own_v.start()
    for part in range(n_x):
        q_load(part).start()
    for part in range(2):
        o_load(part).start()

    own_x.wait()
    hidden = raw[...].astype(jnp.float32)
    factor = lax.rsqrt(jnp.mean(hidden * hidden, axis=-1, keepdims=True) + epsilon)
    xg[me] = (hidden * factor * gain[...]).astype(jnp.bfloat16)

    pl.semaphore_wait(barrier, phase_n + 2)

    def token_copy(block, side, chunk):
        towards = lax.rem(me + 1 - 2 * side + n, n)
        window = pl.ds(pl.multiple_of(chunk * x_tile, x_tile), x_tile)
        return pltpu.make_async_remote_copy(
            src_ref=xg.at[block, :, window],
            dst_ref=xg.at[block, :, window],
            send_sem=x_send.at[side, block, chunk],
            recv_sem=x_recv.at[block, chunk],
            device_id={"tensor": towards},
            device_id_type=MESH,
        )

    for chunk in range(n_x):
        @pl.when(has_right)
        def _():
            token_copy(me, 0, chunk).start()

        @pl.when(has_left)
        def _():
            token_copy(me, 1, chunk).start()

    def exchange(ref, source, send, recv, order, phase):
        bit = order[phase]
        held = [0]
        for earlier in order[:phase]:
            held = held + [slot + earlier for slot in held]
        copies = []
        for slot in held:
            src = source if slot == 0 else ref.at[pl.ds(slot * span, span)]
            copies.append(
                pltpu.make_async_remote_copy(
                    src_ref=src,
                    dst_ref=ref.at[pl.ds((slot + bit) * span, span)],
                    send_sem=send.at[slot + bit],
                    recv_sem=recv.at[slot + bit],
                    device_id={"frame": flip(me_f, bit)},
                    device_id_type=MESH,
                )
            )
        return copies

    phases = [
        exchange(kg, keys, k_send, k_recv, bits, p)
        + exchange(vg, values, v_send, v_recv, v_order, p)
        for p in range(phase_n)
    ]

    def begin(p):
        for copy in phases[p]:
            copy.start()

    def finish(p):
        for copy in phases[p]:
            copy.wait_recv()

    begin(0)

    slot_of = lax.broadcasted_iota(jnp.int32, (1, span), 1)
    pieces = []
    for slot in range(frames_n):
        owner = me_f
        for bit in bits:
            if slot & bit:
                owner = flip(owner, bit)
        pieces.append(slot_of + owner * span)
    frame_index = jnp.concatenate(pieces, axis=1)
    visible_frames = frame_index < frames_n * span - pad[0]

    def q_step(block, side, chunk):
        window = pl.ds(pl.multiple_of(chunk * x_tile, x_tile), x_tile)
        product = jnp.dot(xg[block, :, window], wq[window, :], preferred_element_type=jnp.float32)

        @pl.when(chunk == 0)
        def _():
            qacc[side] = product

        @pl.when(chunk > 0)
        def _():
            qacc[side] += product

        @pl.when(chunk == n_x - 1)
        def _():
            qall[block] = (qacc[side] * HEAD_DIM ** (-0.5)).astype(jnp.bfloat16)

    def own_body(chunk, _):
        q_load(chunk).wait()
        q_step(me, 0, chunk)
        return 0

    lax.fori_loop(0, n_x, own_body, 0)
    for p in range(1, phase_n - 1):
        finish(p - 1)
        begin(p)

    def part_copy(block, side, tile, far=False):
        towards = jnp.where(far, block, lax.rem(me + 1 - 2 * side + n, n))
        slot = jnp.where(far, 1 - side, side)
        window = pl.ds(pl.multiple_of(tile * o_tile, o_tile), o_tile)
        return pltpu.make_async_remote_copy(
            src_ref=pbuf.at[block, :, window],
            dst_ref=rbuf.at[slot, block, :, window],
            send_sem=p_send.at[block, tile],
            recv_sem=p_recv.at[slot, block, tile],
            device_id={"tensor": towards},
            device_id_type=MESH,
        )

    def attend(block, send, side, far):
        block_pos = pos[pl.ds(pl.multiple_of(block * rows, rows), rows), :]
        visible = (frame_index <= block_pos) & visible_frames
        windows = [slice(i, i + HEAD_DIM) for i in range(0, cols, HEAD_DIM)]
        scores = [
            lax.dot_general(
                qall[block, :, window], kg[:, window], (((1,), (1,)), ((), ())),
                preferred_element_type=jnp.float32,
            )
            for window in windows
        ]
        scores = [jnp.where(visible, score, masked_score) for score in scores]
        highest = [jnp.max(score, axis=-1, keepdims=True) for score in scores]
        weights = [
            jnp.where(visible, jnp.exp(score - top), 0.0) for score, top in zip(scores, highest)
        ]
        totals = [jnp.sum(weight, axis=-1, keepdims=True) for weight in weights]
        gathered = [
            jnp.dot(weight.astype(jnp.bfloat16), vg[:, window], preferred_element_type=jnp.float32)
            for weight, window in zip(weights, windows)
        ]
        for window, value, total in zip(windows, gathered, totals):
            abuf[:, window] = (value / total).astype(jnp.bfloat16)

        def o_body(tile, _):
            window = pl.ds(pl.multiple_of(tile * o_tile, o_tile), o_tile)
            pbuf[block, :, window] = jnp.dot(
                abuf[...], wo[:, window], preferred_element_type=jnp.float32
            ).astype(jnp.bfloat16)
            @pl.when(jnp.logical_and(send, tile > 0))
            def _():
                part_copy(block, side, tile - 1, far).start()

            return 0

        lax.fori_loop(0, n_out, o_body, 0)
        @pl.when(send)
        def _():
            part_copy(block, side, n_out - 1, far).start()

    def stage_body(stage, _):
        before = me - stage
        after = me + stage

        def chunk_body(chunk, _):
            @pl.when(before >= 0)
            def _():
                token_copy(before, 0, chunk).wait_recv()

                @pl.when(has_right)
                def _():
                    token_copy(before, 0, chunk).start()

            @pl.when(after < n)
            def _():
                token_copy(after, 1, chunk).wait_recv()

                @pl.when(has_left)
                def _():
                    token_copy(after, 1, chunk).start()

            def side_body(side, _):
                block = me + (2 * side - 1) * stage

                @pl.when(jnp.logical_and(block >= 0, block < n))
                def _():
                    q_step(block, side, chunk)

                return 0

            lax.fori_loop(0, 2, side_body, 0)
            return 0

        lax.fori_loop(0, n_x, chunk_body, 0)

        @pl.when(stage == 1)
        def _():
            if phase_n > 1:
                finish(phase_n - 2)
                begin(phase_n - 1)
            finish(phase_n - 1)
            own_k.wait()
            own_v.wait()
            for part in range(2):
                o_load(part).wait()

        @pl.when(jnp.logical_or(jnp.logical_not(middle), stage == 1))
        def _():
            end_block = jnp.where(has_left, n - 1 - stage, stage)
            near_block = jnp.where(low_half, me + 1, me - 1)
            block = jnp.where(middle, near_block, end_block)
            ends = jnp.logical_not(middle)
            send = jnp.logical_or(ends, starts_sum(block))
            far = jnp.logical_and(ends, stage == n - 1)
            attend(block, send, jnp.where(block > me, 0, 1), far)

        return 0

    def starts_sum(block):
        up = jnp.logical_and(me == 1, block == n - 1)
        down = jnp.logical_and(me == n - 2, block == 0)
        return jnp.logical_or(up, down)

    lax.fori_loop(1, n, stage_body, 0)

    def relay_body(index, _):
        def side_body(turn, _):
            side = jnp.where(low_half, turn, 1 - turn)
            at = index - turn * lag
            known = jnp.logical_and(at >= 0, at < (n - 1) * n_out)
            at = jnp.maximum(at, 0)
            stage = lax.div(at, n_out)
            stage = jnp.where(stage == 0, n - 1, stage)
            tile = lax.rem(at, n_out)
            window = pl.ds(pl.multiple_of(tile * o_tile, o_tile), o_tile)
            block = jnp.where(side == 0, stage, n - 1 - stage)
            passes = jnp.where(side == 0, block > me, block < me)
            passes = jnp.logical_and(passes, jnp.logical_not(starts_sum(block)))

            @pl.when(jnp.logical_and(known, passes))
            def _():
                part_copy(block, side, tile).wait_recv()
                pbuf[block, :, window] = (
                    pbuf[block, :, window].astype(jnp.float32)
                    + rbuf[side, block, :, window].astype(jnp.float32)
                ).astype(jnp.bfloat16)
                part_copy(block, side, tile).start()

            return 0

        lax.fori_loop(0, 2, side_body, 0)
        return 0

    def late_body(index, _):
        step = jnp.where(low_half, index, n - index)
        block = lax.rem(me + step, n)

        @pl.when(jnp.logical_and(middle, index == n))
        def _():
            lax.fori_loop(0, (n - 1) * n_out + lag, relay_body, 0)

        @pl.when(jnp.logical_or(middle, index == n))
        def _():
            send = jnp.logical_and(middle, starts_sum(block))
            attend(block, send, jnp.where(block > me, 0, 1), False)

        return 0

    lax.fori_loop(2, n + 1, late_body, 0)

    def sum_body(tile, _):
        window = pl.ds(pl.multiple_of(tile * o_tile, o_tile), o_tile)

        total = pbuf[me, :, window].astype(jnp.float32)
        for side in range(2):
            part_copy(me, side, tile).wait_recv()
            total = total + rbuf[side, me, :, window].astype(jnp.float32)
        out[:, window] = total.astype(jnp.bfloat16)
        return 0

    lax.fori_loop(0, n_out, sum_body, 0)

    def drain_body(block, _):
        for tile in range(n_out):
            @pl.when(block != me)
            def _():
                part_copy(block, 0, tile).wait_send()

        for chunk in range(n_x):
            @pl.when(jnp.logical_and(has_right, block <= me))
            def _():
                token_copy(block, 0, chunk).wait_send()

            @pl.when(jnp.logical_and(has_left, block >= me))
            def _():
                token_copy(block, 1, chunk).wait_send()

        return 0

    lax.fori_loop(0, n, drain_body, 0)
    for group in phases:
        for copy in group:
            copy.wait_send()


def divisor(total, most):
    return math.gcd(total, most)


def per_device(
    n, frames_n,
    tokens, norm_gain, query_weight, out_weight, cache_keys, cache_values, token_pos, frame_pad
):
    rows, seqs, width = tokens.shape
    cols = query_weight.shape[1]
    span = cache_keys.shape[0]
    x_tile = divisor(width, 1024)
    o_tile = divisor(width, 1024)
    n_x = width // x_tile
    n_out = width // o_tile
    hbm = pl.BlockSpec(memory_space=pl.ANY)
    vmem = pl.BlockSpec(memory_space=pltpu.VMEM)
    bf16 = jnp.bfloat16
    dma = pltpu.SemaphoreType.DMA
    result = pl.pallas_call(
        functools.partial(kernel, n, frames_n, x_tile, o_tile),
        out_shape=jax.ShapeDtypeStruct((rows, width), bf16),
        in_specs=[hbm, vmem, hbm, hbm, hbm, hbm, vmem, pl.BlockSpec(memory_space=pltpu.SMEM)],
        out_specs=vmem,
        scratch_shapes=[
            pltpu.VMEM(query_weight.shape, bf16),
            pltpu.VMEM(out_weight.shape, bf16),
            pltpu.VMEM((frames_n * span, cols), bf16),
            pltpu.VMEM((frames_n * span, cols), bf16),
            pltpu.VMEM((rows, width), bf16),
            pltpu.VMEM((n, rows, width), bf16),
            pltpu.VMEM((2, rows, cols), jnp.float32),
            pltpu.VMEM((n, rows, cols), bf16),
            pltpu.VMEM((rows, cols), bf16),
            pltpu.VMEM((n, rows, width), bf16),
            pltpu.VMEM((2, n, rows, width), bf16),
            dma((n_x,)),
            dma((2,)),
            dma(()),
            dma((2,)),
            dma((frames_n,)),
            dma((frames_n,)),
            dma((frames_n,)),
            dma((frames_n,)),
            dma((2, n, n_x)),
            dma((n, n_x)),
            dma((n, n_out)),
            dma((2, n, n_out)),
        ],
        compiler_params=pltpu.CompilerParams(collective_id=0, has_side_effects=True),
    )(
        tokens.reshape(rows, width),
        norm_gain.reshape(1, width),
        query_weight,
        out_weight,
        cache_keys.reshape(span, cols),
        cache_values.reshape(span, cols),
        token_pos,
        frame_pad,
    )
    return result.reshape(rows, seqs, width)


def solution(mesh):
    placed = (
        P(("frame", "tensor"), None, None),
        P(),
        P(None, "tensor"),
        P("tensor", None),
        P("frame", None, "tensor"),
        P("frame", None, "tensor"),
        P("frame", None),
        P(),
    )
    return jax.shard_map(
        functools.partial(per_device, mesh.shape["tensor"], mesh.shape["frame"]),
        mesh=mesh,
        in_specs=placed,
        out_specs=P(("frame", "tensor"), None, None),
        check_vma=False,
    )
```

```python
import functools
import math

import jax
import jax.numpy as jnp
from jax import lax
from jax.experimental import pallas as pl
from jax.experimental.pallas import tpu as pltpu
from jax.sharding import PartitionSpec as P

HEAD_DIM = 128
epsilon = 1e-06
masked_score = -1e30
MESH = pl.DeviceIdType.MESH


def flip(index, bit):
    return index + bit - 2 * bit * lax.rem(lax.div(index, bit), 2)


def kernel(
    n, frames_n, x_tile, o_tile,
    tok, gain, wq_hbm, wo_hbm, keys, values, pos, pad,
    out,
    wq, wo, kg, vg, pos_col, raw, xg, qacc, qall, abuf, pbuf, rbuf, sums,
    q_sem, o_sem, own_sem, kv_own, k_send, k_recv, v_send, v_recv,
    x_send, x_recv, p_send, p_recv,
):
    me_f = lax.axis_index("frame")
    me = lax.axis_index("tensor")
    rows = tok.shape[0]
    width = tok.shape[1]
    cols = wq.shape[1]
    span = keys.shape[0]
    bits = [1 << b for b in range(int(math.log2(frames_n)))][::-1]
    phase_n = len(bits)
    v_order = bits[1::-1] + bits[2:] if phase_n > 1 else bits
    n_x = width // x_tile
    n_out = width // o_tile
    lag = n_out // 2
    passed = n_out // 2
    has_left = me > 0
    has_right = me < n - 1
    middle = jnp.logical_and(has_left, has_right)
    low_half = 2 * me < n

    def q_load(part):
        window = pl.ds(pl.multiple_of(part * x_tile, x_tile), x_tile)
        return pltpu.make_async_copy(wq_hbm.at[window], wq.at[window], q_sem.at[part])

    def o_load(part):
        depth = cols // 2
        window = pl.ds(part * depth, depth)
        return pltpu.make_async_copy(wo_hbm.at[window], wo.at[window], o_sem.at[part])

    own_x = pltpu.make_async_copy(tok, raw, own_sem)
    own_k = pltpu.make_async_copy(keys, kg.at[pl.ds(0, span)], kv_own.at[0])
    own_v = pltpu.make_async_copy(values, vg.at[pl.ds(0, span)], kv_own.at[1])

    own_x.start()
    barrier = pltpu.get_barrier_semaphore()
    for bit in bits:
        pl.semaphore_signal(
            barrier, inc=1, device_id={"frame": flip(me_f, bit)}, device_id_type=MESH
        )

    @pl.when(has_left)
    def _():
        pl.semaphore_signal(barrier, inc=1, device_id={"tensor": me - 1}, device_id_type=MESH)

    @pl.when(has_right)
    def _():
        pl.semaphore_signal(barrier, inc=1, device_id={"tensor": me + 1}, device_id_type=MESH)

    @pl.when(jnp.logical_not(middle))
    def _():
        pl.semaphore_signal(
            barrier, inc=1, device_id={"tensor": n - 1 - me}, device_id_type=MESH
        )

    own_k.start()
    own_v.start()
    for part in range(n_x):
        q_load(part).start()
    for part in range(2):
        o_load(part).start()

    pos_col[...] = jnp.broadcast_to(pos[...], (HEAD_DIM, n * rows)).T
    own_x.wait()
    hidden = raw[...].astype(jnp.float32)
    factor = lax.rsqrt(jnp.mean(hidden * hidden, axis=-1, keepdims=True) + epsilon)
    xg[me] = (hidden * factor * gain[...]).astype(jnp.bfloat16)

    pl.semaphore_wait(barrier, phase_n + 2)

    def token_copy(block, side, chunk):
        towards = lax.rem(me + 1 - 2 * side + n, n)
        window = pl.ds(pl.multiple_of(chunk * x_tile, x_tile), x_tile)
        return pltpu.make_async_remote_copy(
            src_ref=xg.at[block, :, window],
            dst_ref=xg.at[block, :, window],
            send_sem=x_send.at[side, block, chunk],
            recv_sem=x_recv.at[block, chunk],
            device_id={"tensor": towards},
            device_id_type=MESH,
        )

    for chunk in range(n_x):
        @pl.when(has_right)
        def _():
            token_copy(me, 0, chunk).start()

        @pl.when(has_left)
        def _():
            token_copy(me, 1, chunk).start()

    def exchange(ref, source, send, recv, order, phase):
        bit = order[phase]
        held = [0]
        for earlier in order[:phase]:
            held = held + [slot + earlier for slot in held]
        copies = []
        for slot in held:
            src = source if slot == 0 else ref.at[pl.ds(slot * span, span)]
            copies.append(
                pltpu.make_async_remote_copy(
                    src_ref=src,
                    dst_ref=ref.at[pl.ds((slot + bit) * span, span)],
                    send_sem=send.at[slot + bit],
                    recv_sem=recv.at[slot + bit],
                    device_id={"frame": flip(me_f, bit)},
                    device_id_type=MESH,
                )
            )
        return copies

    phases = [
        exchange(kg, keys, k_send, k_recv, bits, p)
        + exchange(vg, values, v_send, v_recv, v_order, p)
        for p in range(phase_n)
    ]

    def begin(p):
        for copy in phases[p]:
            copy.start()

    def finish(p):
        for copy in phases[p]:
            copy.wait_recv()

    begin(0)

    slot_of = lax.broadcasted_iota(jnp.int32, (1, span), 1)
    pieces = []
    for slot in range(frames_n):
        owner = me_f
        for bit in bits:
            if slot & bit:
                owner = flip(owner, bit)
        pieces.append(slot_of + owner * span)
    frame_index = jnp.concatenate(pieces, axis=1)
    visible_frames = frame_index < frames_n * span - pad[0]

    def q_step(block, side, chunk):
        window = pl.ds(pl.multiple_of(chunk * x_tile, x_tile), x_tile)
        product = jnp.dot(xg[block, :, window], wq[window, :], preferred_element_type=jnp.float32)

        @pl.when(chunk == 0)
        def _():
            qacc[side] = product

        @pl.when(chunk > 0)
        def _():
            qacc[side] += product

        @pl.when(chunk == n_x - 1)
        def _():
            qall[block] = (qacc[side] * HEAD_DIM ** (-0.5)).astype(jnp.bfloat16)

    def own_body(chunk, _):
        q_load(chunk).wait()
        q_step(me, 0, chunk)
        return 0

    lax.fori_loop(0, n_x, own_body, 0)
    for p in range(1, phase_n - 1):
        finish(p - 1)
        begin(p)

    def part_copy(block, side, tile, far=False):
        towards = jnp.where(far, block, lax.rem(me + 1 - 2 * side + n, n))
        slot = jnp.where(far, 1 - side, side)
        window = pl.ds(pl.multiple_of(tile * o_tile, o_tile), o_tile)
        return pltpu.make_async_remote_copy(
            src_ref=pbuf.at[block, :, window],
            dst_ref=rbuf.at[slot, block, :, window],
            send_sem=p_send.at[block, tile],
            recv_sem=p_recv.at[slot, block, tile],
            device_id={"tensor": towards},
            device_id_type=MESH,
        )

    def send_part(block, side, tile, far):
        early = tile < passed
        held = jnp.logical_and(middle, early)

        @pl.when(jnp.logical_not(held))
        def _():
            part_copy(block, side, tile, jnp.logical_and(far, jnp.logical_not(early))).start()

    def attend(block, send, side, far):
        block_pos = pos_col[pl.ds(pl.multiple_of(block * rows, rows), rows), :1]
        visible = (frame_index <= block_pos) & visible_frames
        windows = [slice(i, i + HEAD_DIM) for i in range(0, cols, HEAD_DIM)]
        scores = [
            lax.dot_general(
                qall[block, :, window], kg[:, window], (((1,), (1,)), ((), ())),
                preferred_element_type=jnp.float32,
            )
            for window in windows
        ]
        scores = [jnp.where(visible, score, masked_score) for score in scores]
        highest = [jnp.max(score, axis=-1, keepdims=True) for score in scores]
        weights = [
            jnp.where(visible, jnp.exp(score - top), 0.0) for score, top in zip(scores, highest)
        ]
        totals = [jnp.sum(weight, axis=-1, keepdims=True) for weight in weights]
        gathered = [
            jnp.dot(weight.astype(jnp.bfloat16), vg[:, window], preferred_element_type=jnp.float32)
            for weight, window in zip(weights, windows)
        ]
        for window, value, total in zip(windows, gathered, totals):
            abuf[:, window] = (value / total).astype(jnp.bfloat16)

        def o_body(tile, _):
            window = pl.ds(pl.multiple_of(tile * o_tile, o_tile), o_tile)
            pbuf[block, :, window] = jnp.dot(
                abuf[...], wo[:, window], preferred_element_type=jnp.float32
            ).astype(jnp.bfloat16)
            @pl.when(jnp.logical_and(send, tile > 0))
            def _():
                send_part(block, side, tile - 1, far)

            return 0

        lax.fori_loop(0, n_out, o_body, 0)
        @pl.when(send)
        def _():
            send_part(block, side, n_out - 1, far)

    def stage_body(stage, _):
        before = me - stage
        after = me + stage

        def chunk_body(chunk, _):
            @pl.when(before >= 0)
            def _():
                token_copy(before, 0, chunk).wait_recv()

                @pl.when(has_right)
                def _():
                    token_copy(before, 0, chunk).start()

            @pl.when(after < n)
            def _():
                token_copy(after, 1, chunk).wait_recv()

                @pl.when(has_left)
                def _():
                    token_copy(after, 1, chunk).start()

            def side_body(side, _):
                block = me + (2 * side - 1) * stage

                @pl.when(jnp.logical_and(block >= 0, block < n))
                def _():
                    q_step(block, side, chunk)

                return 0

            lax.fori_loop(0, 2, side_body, 0)
            return 0

        lax.fori_loop(0, n_x, chunk_body, 0)

        @pl.when(stage == 1)
        def _():
            if phase_n > 1:
                finish(phase_n - 2)
                begin(phase_n - 1)
            finish(phase_n - 1)
            own_k.wait()
            own_v.wait()
            for part in range(2):
                o_load(part).wait()

        @pl.when(jnp.logical_or(jnp.logical_not(middle), stage == 1))
        def _():
            end_block = jnp.where(has_left, n - 1 - stage, stage)
            near_block = jnp.where(low_half, me + 1, me - 1)
            block = jnp.where(middle, near_block, end_block)
            ends = jnp.logical_not(middle)
            send = jnp.logical_or(ends, starts_sum(block))
            far = jnp.logical_and(ends, stage == n - 1)
            attend(block, send, jnp.where(block > me, 0, 1), far)

        return 0

    def starts_sum(block):
        up = jnp.logical_and(me == 1, block == n - 1)
        down = jnp.logical_and(me == n - 2, block == 0)
        return jnp.logical_or(up, down)

    lax.fori_loop(1, n, stage_body, 0)

    def relay_body(index, _):
        def side_body(turn, _):
            side = jnp.where(low_half, turn, 1 - turn)
            at = index - turn * lag
            known = jnp.logical_and(at >= 0, at < n * n_out)
            at = jnp.maximum(at, 0)
            stage = lax.div(at, n_out)
            tile = lax.rem(at, n_out)
            known = jnp.logical_and(known, jnp.logical_or(stage > 0, tile >= passed))
            known = jnp.logical_and(known, jnp.logical_or(stage < n - 1, tile < passed))
            stage = jnp.where(stage == 0, n - 1, stage)
            window = pl.ds(pl.multiple_of(tile * o_tile, o_tile), o_tile)
            block = jnp.where(side == 0, stage, n - 1 - stage)
            passes = jnp.where(side == 0, block > me, block < me)
            sent = jnp.logical_and(starts_sum(block), tile >= passed)
            passes = jnp.logical_and(passes, jnp.logical_not(sent))

            @pl.when(jnp.logical_and(known, passes))
            def _():
                part_copy(block, side, tile).wait_recv()
                pbuf[block, :, window] = (
                    pbuf[block, :, window].astype(jnp.float32)
                    + rbuf[side, block, :, window].astype(jnp.float32)
                ).astype(jnp.bfloat16)
                part_copy(block, side, tile).start()

            return 0

        lax.fori_loop(0, 2, side_body, 0)
        return 0

    def late_body(index, _):
        step = jnp.where(low_half, index, n - index)
        block = lax.rem(me + step, n)

        @pl.when(jnp.logical_and(middle, index == n))
        def _():
            lax.fori_loop(0, n * n_out + lag, relay_body, 0)

        @pl.when(jnp.logical_or(middle, index == n))
        def _():
            send = jnp.logical_and(middle, starts_sum(block))
            attend(block, send, jnp.where(block > me, 0, 1), False)

        return 0

    lax.fori_loop(2, n + 1, late_body, 0)

    def sum_body(tile, _):
        window = pl.ds(pl.multiple_of(tile * o_tile, o_tile), o_tile)

        sums[...] = pbuf[me, :, window].astype(jnp.float32)
        for side in range(2):
            from_far = jnp.logical_not(has_right if side else has_left)
            comes = jnp.logical_not(jnp.logical_and(from_far, tile < passed))

            @pl.when(comes)
            def _():
                part_copy(me, side, tile).wait_recv()
                sums[...] += rbuf[side, me, :, window].astype(jnp.float32)

        out[:, window] = sums[...].astype(jnp.bfloat16)
        return 0

    lax.fori_loop(0, n_out, sum_body, 0)

    def drain_body(block, _):
        for tile in range(n_out):
            @pl.when(block != me)
            def _():
                part_copy(block, 0, tile).wait_send()

        for chunk in range(n_x):
            @pl.when(jnp.logical_and(has_right, block <= me))
            def _():
                token_copy(block, 0, chunk).wait_send()

            @pl.when(jnp.logical_and(has_left, block >= me))
            def _():
                token_copy(block, 1, chunk).wait_send()

        return 0

    lax.fori_loop(0, n, drain_body, 0)
    for group in phases:
        for copy in group:
            copy.wait_send()


def divisor(total, most):
    return math.gcd(total, most)


def per_device(
    n, frames_n,
    tokens, norm_gain, query_weight, out_weight, cache_keys, cache_values, token_pos, frame_pad
):
    rows, seqs, width = tokens.shape
    cols = query_weight.shape[1]
    span = cache_keys.shape[0]
    x_tile = divisor(width, 1024)
    o_tile = divisor(width, 1024)
    n_x = width // x_tile
    n_out = width // o_tile
    hbm = pl.BlockSpec(memory_space=pl.ANY)
    vmem = pl.BlockSpec(memory_space=pltpu.VMEM)
    bf16 = jnp.bfloat16
    dma = pltpu.SemaphoreType.DMA
    result = pl.pallas_call(
        functools.partial(kernel, n, frames_n, x_tile, o_tile),
        out_shape=jax.ShapeDtypeStruct((rows, width), bf16),
        in_specs=[hbm, vmem, hbm, hbm, hbm, hbm, vmem, pl.BlockSpec(memory_space=pltpu.SMEM)],
        out_specs=vmem,
        scratch_shapes=[
            pltpu.VMEM(query_weight.shape, bf16),
            pltpu.VMEM(out_weight.shape, bf16),
            pltpu.VMEM((frames_n * span, cols), bf16),
            pltpu.VMEM((frames_n * span, cols), bf16),
            pltpu.VMEM((n * rows, HEAD_DIM), jnp.int32),
            pltpu.VMEM((rows, width), bf16),
            pltpu.VMEM((n, rows, width), bf16),
            pltpu.VMEM((2, rows, cols), jnp.float32),
            pltpu.VMEM((n, rows, cols), bf16),
            pltpu.VMEM((rows, cols), bf16),
            pltpu.VMEM((n, rows, width), bf16),
            pltpu.VMEM((2, n, rows, width), bf16),
            pltpu.VMEM((rows, o_tile), jnp.float32),
            dma((n_x,)),
            dma((2,)),
            dma(()),
            dma((2,)),
            dma((frames_n,)),
            dma((frames_n,)),
            dma((frames_n,)),
            dma((frames_n,)),
            dma((2, n, n_x)),
            dma((n, n_x)),
            dma((n, n_out)),
            dma((2, n, n_out)),
        ],
        compiler_params=pltpu.CompilerParams(collective_id=0, has_side_effects=True),
    )(
        tokens.reshape(rows, width),
        norm_gain.reshape(1, width),
        query_weight,
        out_weight,
        cache_keys.reshape(span, cols),
        cache_values.reshape(span, cols),
        token_pos.reshape(1, n * rows),
        frame_pad,
    )
    return result.reshape(rows, seqs, width)


def solution(mesh):
    placed = (
        P(("frame", "tensor"), None, None),
        P(),
        P(None, "tensor"),
        P("tensor", None),
        P("frame", None, "tensor"),
        P("frame", None, "tensor"),
        P("frame", None),
        P(),
    )
    return jax.shard_map(
        functools.partial(per_device, mesh.shape["tensor"], mesh.shape["frame"]),
        mesh=mesh,
        in_specs=placed,
        out_specs=P(("frame", "tensor"), None, None),
        check_vma=False,
    )
```

```python
import functools
import math

import jax
import jax.numpy as jnp
from jax import lax
from jax.experimental import pallas as pl
from jax.experimental.pallas import tpu as pltpu
from jax.sharding import PartitionSpec as P

HEAD_DIM = 128
epsilon = 1e-06
masked_score = -1e30
MESH = pl.DeviceIdType.MESH


def flip(index, bit):
    return index + bit - 2 * bit * lax.rem(lax.div(index, bit), 2)


def kernel(
    n, frames_n, x_tile, o_tile,
    tok, gain, wq_hbm, wo_hbm, keys, values, pos, pad,
    out,
    wq, wo, kg, vg, pos_col, raw, xg, qacc, qall, abuf, pbuf, rbuf, sums,
    q_sem, o_sem, own_sem, kv_own, k_send, k_recv, v_send, v_recv,
    x_send, x_recv, p_send, p_recv,
):
    me_f = lax.axis_index("frame")
    me = lax.axis_index("tensor")
    rows = tok.shape[0]
    width = tok.shape[1]
    cols = wq.shape[1]
    span = keys.shape[0]
    bits = [1 << b for b in range(int(math.log2(frames_n)))][::-1]
    phase_n = len(bits)
    v_order = bits[1::-1] + bits[2:] if phase_n > 1 else bits
    n_x = width // x_tile
    n_out = width // o_tile
    lag = n_out // 2
    passed = 0
    has_left = me > 0
    has_right = me < n - 1
    middle = jnp.logical_and(has_left, has_right)
    low_half = 2 * me < n

    def q_load(part):
        window = pl.ds(pl.multiple_of(part * x_tile, x_tile), x_tile)
        return pltpu.make_async_copy(wq_hbm.at[window], wq.at[window], q_sem.at[part])

    def o_load(part):
        depth = cols // 2
        window = pl.ds(part * depth, depth)
        return pltpu.make_async_copy(wo_hbm.at[window], wo.at[window], o_sem.at[part])

    own_x = pltpu.make_async_copy(tok, raw, own_sem)
    own_k = pltpu.make_async_copy(keys, kg.at[pl.ds(0, span)], kv_own.at[0])
    own_v = pltpu.make_async_copy(values, vg.at[pl.ds(0, span)], kv_own.at[1])

    own_x.start()
    barrier = pltpu.get_barrier_semaphore()
    for bit in bits:
        pl.semaphore_signal(
            barrier, inc=1, device_id={"frame": flip(me_f, bit)}, device_id_type=MESH
        )

    @pl.when(has_left)
    def _():
        pl.semaphore_signal(barrier, inc=1, device_id={"tensor": me - 1}, device_id_type=MESH)

    @pl.when(has_right)
    def _():
        pl.semaphore_signal(barrier, inc=1, device_id={"tensor": me + 1}, device_id_type=MESH)

    @pl.when(jnp.logical_not(middle))
    def _():
        pl.semaphore_signal(
            barrier, inc=1, device_id={"tensor": n - 1 - me}, device_id_type=MESH
        )

    own_k.start()
    own_v.start()
    for part in range(n_x):
        q_load(part).start()
    for part in range(2):
        o_load(part).start()

    pos_col[...] = jnp.broadcast_to(pos[...], (HEAD_DIM, n * rows)).T
    own_x.wait()
    hidden = raw[...].astype(jnp.float32)
    factor = lax.rsqrt(jnp.mean(hidden * hidden, axis=-1, keepdims=True) + epsilon)
    xg[me] = (hidden * factor * gain[...]).astype(jnp.bfloat16)

    pl.semaphore_wait(barrier, phase_n + 2)

    def token_copy(block, side, chunk):
        towards = lax.rem(me + 1 - 2 * side + n, n)
        window = pl.ds(pl.multiple_of(chunk * x_tile, x_tile), x_tile)
        return pltpu.make_async_remote_copy(
            src_ref=xg.at[block, :, window],
            dst_ref=xg.at[block, :, window],
            send_sem=x_send.at[side, block, chunk],
            recv_sem=x_recv.at[block, chunk],
            device_id={"tensor": towards},
            device_id_type=MESH,
        )

    for chunk in range(n_x):
        @pl.when(has_right)
        def _():
            token_copy(me, 0, chunk).start()

        @pl.when(has_left)
        def _():
            token_copy(me, 1, chunk).start()

    def exchange(ref, source, send, recv, order, phase):
        bit = order[phase]
        held = [0]
        for earlier in order[:phase]:
            held = held + [slot + earlier for slot in held]
        copies = []
        for slot in held:
            src = source if slot == 0 else ref.at[pl.ds(slot * span, span)]
            copies.append(
                pltpu.make_async_remote_copy(
                    src_ref=src,
                    dst_ref=ref.at[pl.ds((slot + bit) * span, span)],
                    send_sem=send.at[slot + bit],
                    recv_sem=recv.at[slot + bit],
                    device_id={"frame": flip(me_f, bit)},
                    device_id_type=MESH,
                )
            )
        return copies

    phases = [
        exchange(kg, keys, k_send, k_recv, bits, p)
        + exchange(vg, values, v_send, v_recv, v_order, p)
        for p in range(phase_n)
    ]

    def begin(p):
        for copy in phases[p]:
            copy.start()

    def finish(p):
        for copy in phases[p]:
            copy.wait_recv()

    begin(0)

    slot_of = lax.broadcasted_iota(jnp.int32, (1, span), 1)
    pieces = []
    for slot in range(frames_n):
        owner = me_f
        for bit in bits:
            if slot & bit:
                owner = flip(owner, bit)
        pieces.append(slot_of + owner * span)
    frame_index = jnp.concatenate(pieces, axis=1)
    visible_frames = frame_index < frames_n * span - pad[0]

    def q_step(block, side, chunk):
        window = pl.ds(pl.multiple_of(chunk * x_tile, x_tile), x_tile)
        product = jnp.dot(xg[block, :, window], wq[window, :], preferred_element_type=jnp.float32)

        @pl.when(chunk == 0)
        def _():
            qacc[side] = product

        @pl.when(chunk > 0)
        def _():
            qacc[side] += product

        @pl.when(chunk == n_x - 1)
        def _():
            qall[block] = (qacc[side] * HEAD_DIM ** (-0.5)).astype(jnp.bfloat16)

    def own_body(chunk, _):
        q_load(chunk).wait()
        q_step(me, 0, chunk)
        return 0

    lax.fori_loop(0, n_x, own_body, 0)
    for p in range(1, phase_n - 1):
        finish(p - 1)
        begin(p)

    def part_copy(block, side, tile, far=False):
        towards = jnp.where(far, block, lax.rem(me + 1 - 2 * side + n, n))
        slot = jnp.where(far, 1 - side, side)
        window = pl.ds(pl.multiple_of(tile * o_tile, o_tile), o_tile)
        return pltpu.make_async_remote_copy(
            src_ref=pbuf.at[block, :, window],
            dst_ref=rbuf.at[slot, block, :, window],
            send_sem=p_send.at[block, tile],
            recv_sem=p_recv.at[slot, block, tile],
            device_id={"tensor": towards},
            device_id_type=MESH,
        )

    def send_part(block, side, tile, far):
        early = tile < passed
        held = jnp.logical_and(middle, early)

        @pl.when(jnp.logical_not(held))
        def _():
            part_copy(block, side, tile, jnp.logical_and(far, jnp.logical_not(early))).start()

    def attend(block, send, side, far):
        block_pos = pos_col[pl.ds(pl.multiple_of(block * rows, rows), rows), :1]
        visible = (frame_index <= block_pos) & visible_frames
        windows = [slice(i, i + HEAD_DIM) for i in range(0, cols, HEAD_DIM)]
        scores = [
            lax.dot_general(
                qall[block, :, window], kg[:, window], (((1,), (1,)), ((), ())),
                preferred_element_type=jnp.float32,
            )
            for window in windows
        ]
        scores = [jnp.where(visible, score, masked_score) for score in scores]
        highest = [jnp.max(score, axis=-1, keepdims=True) for score in scores]
        weights = [
            jnp.where(visible, jnp.exp(score - top), 0.0) for score, top in zip(scores, highest)
        ]
        totals = [jnp.sum(weight, axis=-1, keepdims=True) for weight in weights]
        gathered = [
            jnp.dot(weight.astype(jnp.bfloat16), vg[:, window], preferred_element_type=jnp.float32)
            for weight, window in zip(weights, windows)
        ]
        for window, value, total in zip(windows, gathered, totals):
            abuf[:, window] = (value / total).astype(jnp.bfloat16)

        def o_body(tile, _):
            window = pl.ds(pl.multiple_of(tile * o_tile, o_tile), o_tile)
            pbuf[block, :, window] = jnp.dot(
                abuf[...], wo[:, window], preferred_element_type=jnp.float32
            ).astype(jnp.bfloat16)
            @pl.when(jnp.logical_and(send, tile > 0))
            def _():
                send_part(block, side, tile - 1, far)

            return 0

        lax.fori_loop(0, n_out, o_body, 0)
        @pl.when(send)
        def _():
            send_part(block, side, n_out - 1, far)

    def stage_body(stage, _):
        before = me - stage
        after = me + stage

        def chunk_body(chunk, _):
            @pl.when(before >= 0)
            def _():
                token_copy(before, 0, chunk).wait_recv()

                @pl.when(has_right)
                def _():
                    token_copy(before, 0, chunk).start()

            @pl.when(after < n)
            def _():
                token_copy(after, 1, chunk).wait_recv()

                @pl.when(has_left)
                def _():
                    token_copy(after, 1, chunk).start()

            def side_body(side, _):
                block = me + (2 * side - 1) * stage

                @pl.when(jnp.logical_and(block >= 0, block < n))
                def _():
                    q_step(block, side, chunk)

                return 0

            lax.fori_loop(0, 2, side_body, 0)
            return 0

        lax.fori_loop(0, n_x, chunk_body, 0)

        @pl.when(stage == 1)
        def _():
            if phase_n > 1:
                finish(phase_n - 2)
                begin(phase_n - 1)
            finish(phase_n - 1)
            own_k.wait()
            own_v.wait()
            for part in range(2):
                o_load(part).wait()

        @pl.when(jnp.logical_or(jnp.logical_not(middle), stage == 1))
        def _():
            end_block = jnp.where(has_left, n - 1 - stage, stage)
            near_block = jnp.where(low_half, me + 1, me - 1)
            block = jnp.where(middle, near_block, end_block)
            ends = jnp.logical_not(middle)
            send = jnp.logical_or(ends, starts_sum(block))
            far = jnp.logical_and(ends, stage == n - 1)
            attend(block, send, jnp.where(block > me, 0, 1), far)

        return 0

    def starts_sum(block):
        up = jnp.logical_and(me == 1, block == n - 1)
        down = jnp.logical_and(me == n - 2, block == 0)
        return jnp.logical_or(up, down)

    lax.fori_loop(1, n, stage_body, 0)

    def relay_body(index, _):
        def side_body(turn, _):
            side = jnp.where(low_half, turn, 1 - turn)
            at = index - turn * lag
            known = jnp.logical_and(at >= 0, at < n * n_out)
            at = jnp.maximum(at, 0)
            stage = lax.div(at, n_out)
            tile = lax.rem(at, n_out)
            known = jnp.logical_and(known, jnp.logical_or(stage > 0, tile >= passed))
            known = jnp.logical_and(known, jnp.logical_or(stage < n - 1, tile < passed))
            stage = jnp.where(stage == 0, n - 1, stage)
            window = pl.ds(pl.multiple_of(tile * o_tile, o_tile), o_tile)
            block = jnp.where(side == 0, stage, n - 1 - stage)
            passes = jnp.where(side == 0, block > me, block < me)
            sent = jnp.logical_and(starts_sum(block), tile >= passed)
            passes = jnp.logical_and(passes, jnp.logical_not(sent))

            @pl.when(jnp.logical_and(known, passes))
            def _():
                part_copy(block, side, tile).wait_recv()
                pbuf[block, :, window] = (
                    pbuf[block, :, window].astype(jnp.float32)
                    + rbuf[side, block, :, window].astype(jnp.float32)
                ).astype(jnp.bfloat16)
                part_copy(block, side, tile).start()

            return 0

        lax.fori_loop(0, 2, side_body, 0)
        return 0

    def late_body(index, _):
        step = jnp.where(low_half, index, n - index)
        block = lax.rem(me + step, n)

        @pl.when(jnp.logical_and(middle, index == n))
        def _():
            lax.fori_loop(0, n * n_out + lag, relay_body, 0)

        @pl.when(jnp.logical_or(middle, index == n))
        def _():
            send = jnp.logical_and(middle, starts_sum(block))
            attend(block, send, jnp.where(block > me, 0, 1), False)

        return 0

    lax.fori_loop(2, n + 1, late_body, 0)

    def sum_body(tile, _):
        window = pl.ds(pl.multiple_of(tile * o_tile, o_tile), o_tile)

        sums[...] = pbuf[me, :, window].astype(jnp.float32)
        for side in range(2):
            from_far = jnp.logical_not(has_right if side else has_left)
            comes = jnp.logical_not(jnp.logical_and(from_far, tile < passed))

            @pl.when(comes)
            def _():
                part_copy(me, side, tile).wait_recv()
                sums[...] += rbuf[side, me, :, window].astype(jnp.float32)

        out[:, window] = sums[...].astype(jnp.bfloat16)
        return 0

    lax.fori_loop(0, n_out, sum_body, 0)

    def drain_body(block, _):
        for tile in range(n_out):
            @pl.when(block != me)
            def _():
                part_copy(block, 0, tile).wait_send()

        for chunk in range(n_x):
            @pl.when(jnp.logical_and(has_right, block <= me))
            def _():
                token_copy(block, 0, chunk).wait_send()

            @pl.when(jnp.logical_and(has_left, block >= me))
            def _():
                token_copy(block, 1, chunk).wait_send()

        return 0

    lax.fori_loop(0, n, drain_body, 0)
    for group in phases:
        for copy in group:
            copy.wait_send()


def divisor(total, most):
    return math.gcd(total, most)


def per_device(
    n, frames_n,
    tokens, norm_gain, query_weight, out_weight, cache_keys, cache_values, token_pos, frame_pad
):
    rows, seqs, width = tokens.shape
    cols = query_weight.shape[1]
    span = cache_keys.shape[0]
    x_tile = divisor(width, 1024)
    o_tile = divisor(width, 1024)
    n_x = width // x_tile
    n_out = width // o_tile
    hbm = pl.BlockSpec(memory_space=pl.ANY)
    vmem = pl.BlockSpec(memory_space=pltpu.VMEM)
    bf16 = jnp.bfloat16
    dma = pltpu.SemaphoreType.DMA
    result = pl.pallas_call(
        functools.partial(kernel, n, frames_n, x_tile, o_tile),
        out_shape=jax.ShapeDtypeStruct((rows, width), bf16),
        in_specs=[hbm, vmem, hbm, hbm, hbm, hbm, vmem, pl.BlockSpec(memory_space=pltpu.SMEM)],
        out_specs=vmem,
        scratch_shapes=[
            pltpu.VMEM(query_weight.shape, bf16),
            pltpu.VMEM(out_weight.shape, bf16),
            pltpu.VMEM((frames_n * span, cols), bf16),
            pltpu.VMEM((frames_n * span, cols), bf16),
            pltpu.VMEM((n * rows, HEAD_DIM), jnp.int32),
            pltpu.VMEM((rows, width), bf16),
            pltpu.VMEM((n, rows, width), bf16),
            pltpu.VMEM((2, rows, cols), jnp.float32),
            pltpu.VMEM((n, rows, cols), bf16),
            pltpu.VMEM((rows, cols), bf16),
            pltpu.VMEM((n, rows, width), bf16),
            pltpu.VMEM((2, n, rows, width), bf16),
            pltpu.VMEM((rows, o_tile), jnp.float32),
            dma((n_x,)),
            dma((2,)),
            dma(()),
            dma((2,)),
            dma((frames_n,)),
            dma((frames_n,)),
            dma((frames_n,)),
            dma((frames_n,)),
            dma((2, n, n_x)),
            dma((n, n_x)),
            dma((n, n_out)),
            dma((2, n, n_out)),
        ],
        compiler_params=pltpu.CompilerParams(collective_id=0, has_side_effects=True),
    )(
        tokens.reshape(rows, width),
        norm_gain.reshape(1, width),
        query_weight,
        out_weight,
        cache_keys.reshape(span, cols),
        cache_values.reshape(span, cols),
        token_pos.reshape(1, n * rows),
        frame_pad,
    )
    return result.reshape(rows, seqs, width)


def solution(mesh):
    placed = (
        P(("frame", "tensor"), None, None),
        P(),
        P(None, "tensor"),
        P("tensor", None),
        P("frame", None, "tensor"),
        P("frame", None, "tensor"),
        P("frame", None),
        P(),
    )
    return jax.shard_map(
        functools.partial(per_device, mesh.shape["tensor"], mesh.shape["frame"]),
        mesh=mesh,
        in_specs=placed,
        out_specs=P(("frame", "tensor"), None, None),
        check_vma=False,
    )
```
